32 devices in a mesh: dp: 8 (over z, y), mp: 4 (over x, core).
Axes of the slice: x: 2, y: 2, z: 4, core: 2. Of those that a mesh axis runs over, the one named last changes fastest.
Arguments:
- tokens: bfloat16 [1024, 2048], P('dp', 'mp'), may hold values from -6 to 6
- expand_weight: bfloat16 [8, 256, 1024], P('mp'), may hold values from -0.375 to 0.375
- section_weight: bfloat16 [2, 32, 2, 256, 256], P(None, 'mp'), may hold values from -0.25 to 0.25
- contract_weight: bfloat16 [8, 1024, 256], P('mp'), may hold values from -0.1875 to 0.1875
- pattern: int32 [2, 8], replicated, may hold values from 0 to 7, each once within a row
- cotangent: bfloat16 [1024, 2048], P('dp', 'mp'), may hold values from -6 to 6
Outputs:
- output: bfloat16 [1024, 2048], P('dp', 'mp')
- input_grad: bfloat16 [1024, 2048], P('dp', 'mp')
- expand_grad: bfloat16 [8, 256, 1024], P('mp', 'dp')
- section_grad: bfloat16 [2, 32, 2, 256, 256], P(None, 'mp', None, 'dp')
- contract_grad: bfloat16 [8, 1024, 256], P('mp', 'dp')
The draws below stay inside these ranges and needn't reach their ends.
Inputs may be any that keep to these rules, and one draw needn't show every extreme that they name: Each row of pattern is a permutation of 0 .. 7.
All inputs are finite; a program needn't handle non-finite values.
Results may differ from the reference program's by a relative error of at most 0.025.
Values may be sent and summed in bfloat16 or wider, within the bound.
No kernel may reach another device: no remote copies, remote signals or barrier semaphores. Data moves between devices by JAX's collectives and lax.ppermute only.
A program may use at most 128 MiB of HBM per device.

```python
import math
import jax
import jax.numpy as jnp
from jax import lax

BLK = 256
EXPAND = 4
TOK_DEV = 128
HB_DEV = 8
SECTIONS = 2
IB = 8
NB = 32
D = 2048
TOKENS = 1024
N_DP = 8


def level_of(stream_key, dims, cuts, low, largest):
    def one(axis_at, shards_of):
        draws = jax.random.uniform(jax.random.fold_in(jax.random.fold_in(stream_key, 6), axis_at), (shards_of,), jnp.float32, low / len(cuts), largest / len(cuts))
        return jnp.repeat(jnp.exp(draws), dims[axis_at] // shards_of).reshape((-1,) + (1,) * (len(dims) - axis_at - 1))

    level = one(*cuts[0])
    for cut in cuts[1:]:
        level = level * one(*cut)
    return level


def normal_values(own_key, extent, width, bound, split=(), kind=jnp.bfloat16):
    level = level_of(own_key, extent, split, -0.22, 0.18) if split else 1.0
    drawn = jax.random.normal(own_key, extent, jnp.float32) * width * level
    return jnp.minimum(jnp.maximum(drawn, -bound), bound).astype(kind)


def setup_inputs(seed: int = 0) -> dict:
    key_of = jax.random.split(jax.random.key(seed), 7)
    tokens = normal_values(key_of[0], (TOKENS, D), 1.0, 6.0, ((0, 8), (1, 4)))
    expand_weight = normal_values(key_of[1], (IB, BLK, EXPAND * BLK), BLK ** -0.5, 0.375, ((0, 4),))
    section_weight = normal_values(key_of[2], (SECTIONS, NB, 2, BLK, BLK), (2 * BLK) ** -0.5, 0.25, ((1, 4),))
    contract_weight = normal_values(key_of[3], (IB, EXPAND * BLK, BLK), (EXPAND * BLK) ** -0.5, 0.1875, ((0, 4),))
    pattern = jax.vmap(lambda own: jax.random.permutation(own, HB_DEV))(jax.random.split(key_of[4], SECTIONS)).reshape((SECTIONS, HB_DEV)).astype(jnp.int32)
    cotangent = normal_values(key_of[5], (TOKENS, D), 1.0, 6.0, ((0, 8), (1, 4)))
    return dict(tokens=tokens, expand_weight=expand_weight, section_weight=section_weight, contract_weight=contract_weight, pattern=pattern, cotangent=cotangent)


def gelu_exact(values):
    return jax.nn.gelu(values, approximate=False)

def group_pass(tok_rows_in, cot_rows_in, expand_weight, section_weight, contract_weight, pattern):
    row_count = tok_rows_in.shape[0]
    tok_blocks = tok_rows_in.reshape(row_count, IB, BLK).astype(jnp.float32)
    expand_full = expand_weight.astype(jnp.float32)
    hidden = jnp.einsum('rmi,mio->rmo', tok_blocks, expand_full).reshape(row_count, NB, BLK).astype(jnp.bfloat16)
    block_ids = jnp.arange(NB, dtype=jnp.int32)
    owner_dev = block_ids // HB_DEV
    within = block_ids % HB_DEV
    saved = []
    mixed = None
    for section in range(SECTIONS):
        stride = HB_DEV * 2 ** section
        source = (owner_dev * HB_DEV + pattern[section][within]).astype(jnp.int32)
        paired = jnp.stack([hidden[:, source], hidden[:, jnp.bitwise_xor(source, stride)]], axis=2)
        saved.append(paired)
        mixed = jnp.einsum('rbsc,bscd->rbd', paired.astype(jnp.float32), section_weight[section].astype(jnp.float32))
        if section + 1 < SECTIONS:
            hidden = mixed.astype(jnp.bfloat16)
    activated, gelu_back = jax.vjp(gelu_exact, mixed)
    activated = activated.astype(jnp.bfloat16)
    gelu_blocks = activated.reshape(row_count, IB, EXPAND * BLK).astype(jnp.float32)
    contract_full = contract_weight.astype(jnp.float32)
    output = jnp.einsum('rje,jed->rjd', gelu_blocks, contract_full).reshape(row_count, D).astype(jnp.bfloat16)
    cot_blocks = cot_rows_in.reshape(row_count, IB, BLK).astype(jnp.float32)
    contract_term = jnp.einsum('rje,rjd->jed', gelu_blocks, cot_blocks)
    gelu_grad = jnp.einsum('rjd,jed->rje', cot_blocks, contract_full).reshape(row_count, NB, BLK)
    upstream = gelu_back(gelu_grad)[0].astype(jnp.bfloat16)
    section_terms = [None] * SECTIONS
    for section in reversed(range(SECTIONS)):
        stride = HB_DEV * 2 ** section
        up_full = upstream.astype(jnp.float32)
        section_terms[section] = jnp.einsum('rbsc,rbd->bscd', saved[section].astype(jnp.float32), up_full)
        local_part = jnp.einsum('rbd,bcd->rbc', up_full, section_weight[section, :, 0].astype(jnp.float32))
        far_part = jnp.einsum('rbd,bcd->rbc', up_full, section_weight[section, :, 1].astype(jnp.float32)).astype(jnp.bfloat16)
        inverse = jnp.argsort(pattern[section]).astype(jnp.int32)
        target = (owner_dev * HB_DEV + inverse[within]).astype(jnp.int32)
        upstream = (local_part[:, target] + far_part[:, jnp.bitwise_xor(target, stride)].astype(jnp.float32)).astype(jnp.bfloat16)
    first_grad = upstream.reshape(row_count, IB, EXPAND * BLK).astype(jnp.float32)
    expand_term = jnp.einsum('rmi,rmo->mio', tok_blocks, first_grad)
    input_grad = jnp.einsum('rmo,mio->rmi', first_grad, expand_full).reshape(row_count, D).astype(jnp.bfloat16)
    return (output, input_grad, jnp.stack(section_terms), expand_term, contract_term)

def reference(tokens, expand_weight, section_weight, contract_weight, pattern, cotangent):
    outputs = []
    input_grads = []
    totals = []
    for group_idx in range(N_DP):
        row_start = group_idx * TOK_DEV
        result = group_pass(tokens[row_start:row_start + TOK_DEV], cotangent[row_start:row_start + TOK_DEV], expand_weight, section_weight, contract_weight, pattern)
        outputs.append(result[0])
        input_grads.append(result[1])
        rounded = [lax.optimization_barrier(partial_term.astype(jnp.bfloat16)).astype(jnp.float32) for partial_term in result[2:]]
        if group_idx == 0:
            totals = rounded
        else:
            totals = [summed + extra for summed, extra in zip(totals, rounded)]
    grad_scale = 1.0 / math.sqrt(TOKENS)
    return (jnp.concatenate(outputs, axis=0), jnp.concatenate(input_grads, axis=0), (totals[1] * grad_scale).astype(jnp.bfloat16), (totals[0] * grad_scale).astype(jnp.bfloat16), (totals[2] * grad_scale).astype(jnp.bfloat16))
```

```python
import functools
import math

import jax
import jax.numpy as jnp
from jax import lax
from jax.experimental import pallas as pl
from jax.experimental.pallas import tpu as pltpu
from jax.sharding import PartitionSpec as P

F32 = jnp.float32
BF16 = jnp.bfloat16
NN = (((1,), (0,)), ((), ()))
NT = (((1,), (1,)), ((), ()))
SMEM = pl.BlockSpec(memory_space=pltpu.SMEM)
VMEM = pl.BlockSpec(memory_space=pltpu.VMEM)


def mm(left, right, dims=NN):
    return lax.dot_general(left, right, dims, preferred_element_type=F32)


def call(kernel, name, ins, outs, smem=0, scratch=()):
    specs = [SMEM] * smem + [VMEM] * (len(ins) - smem)
    return pl.pallas_call(
        kernel,
        out_shape=[jax.ShapeDtypeStruct(shape, kind) for shape, kind in outs],
        in_specs=specs,
        out_specs=[VMEM] * len(outs),
        scratch_shapes=list(scratch),
        name=name,
    )(*ins)


def expand_kernel(pattern, tok, weight, chosen, place):
    feats, blk, wide = weight.shape
    per = wide // blk
    for at in range(feats * per):
        place[pattern[0, at]] = at
    for j in range(feats):
        full = mm(tok[:, j * blk : (j + 1) * blk], weight[j])
        for q in range(per):
            chosen[place[j * per + q]] = full[:, q * blk : (q + 1) * blk].astype(BF16)


def mix_kernel(section, pattern, chosen, partner, weight, *outs):
    at = 0
    for out in outs:
        for l in range(out.shape[0]):
            b = pattern[section + 1, at]
            mixed = mm(chosen[b], weight[b, 0]) + mm(partner[b], weight[b, 1])
            out[l] = mixed.astype(BF16)
            at += 1


def gelu_grad_kernel(cot, weight, out):
    feats, wide, blk = weight.shape
    per = wide // blk
    for j in range(feats):
        for q in range(per):
            out[j * per + q] = mm(
                cot[:, j * blk : (j + 1) * blk], weight[j, q * blk : (q + 1) * blk, :], NT
            )


def last_kernel(base, own, partner, weight, grad, act, up, outgoing):
    for l in range(own.shape[0]):
        z = mm(own[l], weight[base + l, 0]) + mm(partner[l], weight[base + l, 1])
        phi = 0.5 + 0.5 * lax.erf(z * math.sqrt(0.5))
        act[l] = (z * phi).astype(BF16)
        slope = phi + z * (jnp.exp(-0.5 * z * z) * (1.0 / math.sqrt(2.0 * math.pi)))
        g = (grad[base + l] * slope).astype(BF16)
        up[l] = g
        outgoing[l] = mm(g, weight[base + l, 1], NT).astype(BF16)


def halves_matrix(side, blk, chunk):
    row = lax.broadcasted_iota(jnp.int32, (blk, blk), 0)
    col = lax.broadcasted_iota(jnp.int32, (blk, blk), 1)
    half = blk // 2
    first = row < half
    inner = jnp.where(first, row, row - half)
    pick = jnp.where(first, side, 1 - side)
    shift = chunk.bit_length() - 1
    want = ((inner >> shift) << (shift + 1)) + pick * chunk + (inner & (chunk - 1))
    return jnp.where(col == want, 1.0, 0.0).astype(BF16)


def halves_kernel(chunk, count, side, *refs):
    keep, send = refs[count], refs[count + 1]
    blk = refs[0].shape[-1] if len(refs[0].shape) == 3 else 2 * keep.shape[1]
    pick = halves_matrix(side[0], blk, chunk)
    half = blk // 2
    at = 0
    for ref in refs[:count]:
        if len(ref.shape) == 3:
            parts = [ref[l] for l in range(ref.shape[0])]
        else:
            parts = [ref[:, l * blk : (l + 1) * blk] for l in range(ref.shape[1] // blk)]
        for part in parts:
            turned = mm(pick, part, NT).astype(BF16)
            keep[at] = turned[:half]
            send[at] = turned[half:]
            at += 1


def split_halves(side, chunk, name, *blocks):
    tok = blocks[0].shape[-2]
    blk = 256 if blocks[0].ndim == 2 else blocks[0].shape[-1]
    count = sum(x.shape[0] if x.ndim == 3 else x.shape[1] // blk for x in blocks)
    shape = (count, blk // 2, tok)
    return call(
        functools.partial(halves_kernel, chunk, len(blocks)),
        name,
        (side,) + blocks,
        [(shape, BF16)] * 2,
        smem=1,
    )


def section_term_kernel(ways, *refs):
    keeps, comes = refs[:2 * ways], refs[2 * ways : 4 * ways]
    ups, up_comes = refs[4 * ways : 5 * ways], refs[5 * ways : 6 * ways]
    out = refs[6 * ways]
    pieces, _, _, chunk, _ = out.shape
    at = 0
    for w in range(ways):
        for l in range(ups[w].shape[0]):
            right = jnp.concatenate([ups[w][l], up_comes[w][l]], axis=0)
            for s in range(2):
                left = jnp.concatenate(
                    [keeps[s * ways + w][l], comes[s * ways + w][l]], axis=1
                )
                term = mm(left, right).astype(BF16)
                for piece in range(pieces):
                    out[piece, at, s] = term[piece * chunk : (piece + 1) * chunk]
            at += 1


def expand_term_kernel(keep, come, up, up_come, out):
    pieces, feats, chunk, wide = out.shape
    blk = up.shape[-1]
    per = wide // blk
    for j in range(feats):
        left = jnp.concatenate([keep[j], come[j]], axis=1)
        for q in range(per):
            right = jnp.concatenate([up[j * per + q], up_come[j * per + q]], axis=0)
            term = mm(left, right).astype(BF16)
            for piece in range(pieces):
                out[piece, j, :, q * blk : (q + 1) * blk] = term[
                    piece * chunk : (piece + 1) * chunk
                ]


def contract_term_kernel(ways, *refs):
    keeps, comes = refs[:ways], refs[ways : 2 * ways]
    cot, cot_come, out = refs[2 * ways :]
    pieces, feats, chunk, blk = out.shape
    half = keeps[0].shape[1]
    per = pieces * chunk // half
    at = 0
    for w in range(ways):
        for l in range(keeps[w].shape[0]):
            j, q = at // per, at % per
            left = jnp.concatenate([keeps[w][l], comes[w][l]], axis=1)
            cols = slice(j * blk, (j + 1) * blk)
            right = jnp.concatenate([cot[:, cols], cot_come[:, cols]], axis=0)
            term = mm(left, right).astype(BF16)
            for part in range(half // chunk):
                out[q * (half // chunk) + part, j] = term[part * chunk : (part + 1) * chunk]
            at += 1


def output_kernel(ways, *refs):
    acts, weight, out = refs[:ways], refs[ways], refs[ways + 1]
    feats, wide, blk = weight.shape
    per = wide // blk
    blocks = [act[l] for act in acts for l in range(act.shape[0])]
    for j in range(feats):
        full = jnp.concatenate(blocks[j * per : (j + 1) * per], axis=1)
        out[:, j * blk : (j + 1) * blk] = mm(full, weight[j]).astype(BF16)


def back_kernel(section, ways, pattern, *refs):
    ups, arrived = refs[:ways], refs[ways : 2 * ways]
    weight, before, grad, outgoing, local = refs[2 * ways :]
    at = 0
    for w in range(ways):
        for l in range(ups[w].shape[0]):
            b = pattern[section, at]
            total = mm(ups[w][l], weight[at, 0], NT) + arrived[w][l].astype(F32)
            g = total.astype(BF16)
            grad[b] = g
            outgoing[b] = mm(g, before[b, 1], NT).astype(BF16)
            local[b] = mm(g, before[b, 0], NT)
            at += 1


def back_next_kernel(section, pattern, local_in, arrived, before, grad, outgoing, local):
    for at in range(local_in.shape[0]):
        b = pattern[section, at]
        g = (local_in[at] + arrived[at].astype(F32)).astype(BF16)
        grad[b] = g
        outgoing[b] = mm(g, before[b, 1], NT).astype(BF16)
        local[b] = mm(g, before[b, 0], NT)


def first_kernel(pattern, local_in, arrived, weight, grad, out):
    feats, blk, wide = weight.shape
    per = wide // blk
    for at in range(feats * per):
        b = pattern[0, at]
        grad[b] = (local_in[at] + arrived[at].astype(F32)).astype(BF16)
    for j in range(feats):
        full = jnp.concatenate([grad[j * per + q] for q in range(per)], axis=1)
        out[:, j * blk : (j + 1) * blk] = mm(full, weight[j], NT).astype(BF16)


def swap(value, axis, step):
    return lax.ppermute(value, axis, [(i, i ^ step) for i in range(lax.axis_size(axis))])


def line_reduce(parts, spot, groups):
    def at(index):
        index = jnp.clip(index, 0, groups - 1)
        return lax.dynamic_index_in_dim(parts, index, 0, keepdims=False)

    up = down = None
    for step in range(1, groups):
        right = at(spot + groups - step)
        left = at(spot - groups + step)
        if up is not None:
            right = (right.astype(F32) + up.astype(F32)).astype(BF16)
            left = (left.astype(F32) + down.astype(F32)).astype(BF16)
        pairs = [(i, i + 1) for i in range(step)]
        pairs = [(2 * a + y, 2 * b + y) for a, b in pairs for y in range(2)]
        back = [(groups - 1 - i, groups - 2 - i) for i in range(step)]
        back = [(2 * a + y, 2 * b + y) for a, b in back for y in range(2)]
        up = lax.ppermute(right, "dp", pairs)
        down = lax.ppermute(left, "dp", back)
    own = at(spot).astype(F32)
    if up is None:
        return own
    return own + up.astype(F32) + down.astype(F32)


def body(tokens, expand_weight, section_weight, contract_weight, pattern, cotangent):
    rows = tokens.shape[0]
    feats, blk, wide = expand_weight.shape
    sections, count = section_weight.shape[:2]
    copies = lax.axis_size("dp")
    groups = copies // 2
    scale = 1.0 / math.sqrt(rows * copies)
    place = lax.axis_index("dp")
    side = (place % 2).astype(jnp.int32).reshape(1)
    spot = place // 2
    narrow = blk // copies
    tall = wide // copies
    ways = 2
    cut = count // ways
    block = (count, rows, blk)
    part = (cut, rows, blk)
    weights = [section_weight[k] for k in range(sections)]
    last = sections - 1

    cot_come = swap(cotangent, "dp", 1)
    place_mem = pltpu.SMEM((count,), jnp.int32)
    (chosen,) = call(
        expand_kernel, "expand", (pattern, tokens, expand_weight), [(block, BF16)],
        smem=1, scratch=(place_mem,),
    )
    tok_keep, tok_send = split_halves(side, narrow, "tok_halves", tokens)
    tok_come = swap(tok_send, "dp", 1)
    saved = []
    for k in range(last):
        partner = swap(chosen, "mp", 1 << k)
        final = k + 1 == last
        outs = call(
            functools.partial(mix_kernel, k), f"mix{k}",
            (pattern, chosen, partner, weights[k]),
            [(part, BF16)] * ways if final else [(block, BF16)], smem=1,
        )
        own_keep, own_send = split_halves(side, narrow, f"halves_own{k}", chosen)
        own_come = swap(own_send, "dp", 1)
        par_keep, par_send = split_halves(side, narrow, f"halves_par{k}", partner)
        par_come = swap(par_send, "dp", 1)
        saved.append(((own_keep, par_keep), (own_come, par_come)))
        chosen = outs if final else outs[0]
    partners = [swap(x, "mp", 1 << last) for x in chosen]
    (grad_in,) = call(gelu_grad_kernel, "gelu_grad", (cotangent, contract_weight), [(block, F32)])
    own_half = [split_halves(side, narrow, f"own_last{w}", chosen[w]) for w in range(ways)]
    own_come = [swap(x[1], "dp", 1) for x in own_half]
    acts, ups, outgoing, arrived = [], [], [], []
    for w in range(ways):
        a, u, o = call(
            functools.partial(last_kernel, w * cut), f"last{w}",
            (chosen[w], partners[w], weights[last], grad_in), [(part, BF16)] * 3,
        )
        acts.append(a)
        ups.append(u)
        arrived.append(swap(o, "mp", 1 << last))
    act_half = [split_halves(side, tall, f"act{w}", acts[w]) for w in range(ways)]
    act_come = [swap(x[1], "dp", 1) for x in act_half]
    up_come = [swap(u, "dp", 1) for u in ups]
    par_half = [split_halves(side, narrow, f"par_last{w}", partners[w]) for w in range(ways)]
    par_come = [swap(x[1], "dp", 1) for x in par_half]

    (contract_parts,) = call(
        functools.partial(contract_term_kernel, ways), "contract_term",
        tuple(x[0] for x in act_half) + tuple(act_come) + (cotangent, cot_come),
        [((groups, feats, tall, blk), BF16)],
    )
    contract_sum = line_reduce(contract_parts, spot, groups)
    section_shape = (groups, count, 2, narrow, blk)
    (last_parts,) = call(
        functools.partial(section_term_kernel, ways), "section_term_last",
        tuple(x[0] for x in own_half) + tuple(x[0] for x in par_half)
        + tuple(own_come) + tuple(par_come) + tuple(ups) + tuple(up_come),
        [(section_shape, BF16)],
    )
    section_sums = [None] * sections
    section_sums[last] = line_reduce(last_parts, spot, groups)

    local = None
    for k in range(last, 0, -1):
        if k == last:
            grad, out, local = call(
                functools.partial(back_kernel, k, ways), f"back{k}",
                (pattern,) + tuple(ups) + tuple(arrived) + (weights[k], weights[k - 1]),
                [(block, BF16), (block, BF16), (block, F32)], smem=1,
            )
        else:
            grad, out, local = call(
                functools.partial(back_next_kernel, k), f"back{k}",
                (pattern, local, come, weights[k - 1]),
                [(block, BF16), (block, BF16), (block, F32)], smem=1,
            )
        come = swap(out, "mp", 1 << (k - 1))
        grad_come = swap(grad, "dp", 1)
        keeps, comes = saved[k - 1]
        (parts,) = call(
            functools.partial(section_term_kernel, 1), f"section_term{k - 1}",
            keeps + comes + (grad, grad_come), [(section_shape, BF16)],
        )
        section_sums[k - 1] = line_reduce(parts, spot, groups)
    first_grad, input_grad = call(
        first_kernel, "first", (pattern, local, come, expand_weight),
        [(block, BF16), ((rows, feats * blk), BF16)], smem=1,
    )
    first_come = swap(first_grad, "dp", 1)
    (output,) = call(
        functools.partial(output_kernel, ways), "output", tuple(acts) + (contract_weight,),
        [((rows, feats * blk), BF16)],
    )
    (expand_parts,) = call(
        expand_term_kernel, "expand_term", (tok_keep, tok_come, first_grad, first_come),
        [((groups, feats, narrow, wide), BF16)],
    )
    expand_sum = line_reduce(expand_parts, spot, groups)
    section_grad = (jnp.stack(section_sums) * scale).astype(BF16)
    expand_grad = (expand_sum * scale).astype(BF16)
    contract_grad = (contract_sum * scale).astype(BF16)
    return (output, input_grad, expand_grad, section_grad, contract_grad)


def solution(mesh):
    return jax.shard_map(
        body,
        mesh=mesh,
        in_specs=(
            P("dp", "mp"),
            P("mp", None, None),
            P(None, "mp", None, None, None),
            P("mp", None, None),
            P(),
            P("dp", "mp"),
        ),
        out_specs=(
            P("dp", "mp"),
            P("dp", "mp"),
            P("mp", "dp", None),
            P(None, "mp", None, "dp", None),
            P("mp", "dp", None),
        ),
        check_vma=False,
    )
```

```python
import functools
import math

import jax
import jax.numpy as jnp
from jax import lax
from jax.experimental import pallas as pl
from jax.experimental.pallas import tpu as pltpu
from jax.sharding import PartitionSpec as P

F32 = jnp.float32
BF16 = jnp.bfloat16
NN = (((1,), (0,)), ((), ()))
NT = (((1,), (1,)), ((), ()))
SMEM = pl.BlockSpec(memory_space=pltpu.SMEM)
VMEM = pl.BlockSpec(memory_space=pltpu.VMEM)


def mm(left, right, dims=NN):
    return lax.dot_general(left, right, dims, preferred_element_type=F32)


def call(kernel, name, ins, outs, smem=0, scratch=(), limit=12):
    specs = [SMEM] * smem + [VMEM] * (len(ins) - smem)
    return pl.pallas_call(
        kernel,
        out_shape=[jax.ShapeDtypeStruct(shape, kind) for shape, kind in outs],
        in_specs=specs,
        out_specs=[VMEM] * len(outs),
        scratch_shapes=list(scratch),
        name=name,
        compiler_params=pltpu.CompilerParams(vmem_limit_bytes=limit << 20),
    )(*ins)


def expand_kernel(pattern, tok, weight, chosen, place):
    feats, blk, wide = weight.shape
    per = wide // blk
    for at in range(feats * per):
        place[pattern[0, at]] = at
    for j in range(feats):
        full = mm(tok[:, j * blk : (j + 1) * blk], weight[j])
        for q in range(per):
            chosen[place[j * per + q]] = full[:, q * blk : (q + 1) * blk].astype(BF16)


def mix_kernel(section, pattern, chosen, partner, weight, *outs):
    at = 0
    for out in outs:
        for l in range(out.shape[0]):
            b = pattern[section + 1, at]
            mixed = mm(chosen[b], weight[b, 0]) + mm(partner[b], weight[b, 1])
            out[l] = mixed.astype(BF16)
            at += 1


def gelu_grad_kernel(cot, weight, out):
    feats, wide, blk = weight.shape
    per = wide // blk
    for j in range(feats):
        for q in range(per):
            out[j * per + q] = mm(
                cot[:, j * blk : (j + 1) * blk], weight[j, q * blk : (q + 1) * blk, :], NT
            )


def last_kernel(base, own, partner, weight, grad, act, up, outgoing):
    for l in range(own.shape[0]):
        z = mm(own[l], weight[base + l, 0]) + mm(partner[l], weight[base + l, 1])
        phi = 0.5 + 0.5 * lax.erf(z * math.sqrt(0.5))
        act[l] = (z * phi).astype(BF16)
        slope = phi + z * (jnp.exp(-0.5 * z * z) * (1.0 / math.sqrt(2.0 * math.pi)))
        g = (grad[base + l] * slope).astype(BF16)
        up[l] = g
        outgoing[l] = mm(g, weight[base + l, 1], NT).astype(BF16)


def halves_matrix(side, blk, chunk):
    row = lax.broadcasted_iota(jnp.int32, (blk, blk), 0)
    col = lax.broadcasted_iota(jnp.int32, (blk, blk), 1)
    half = blk // 2
    first = row < half
    inner = jnp.where(first, row, row - half)
    pick = jnp.where(first, side, 1 - side)
    shift = chunk.bit_length() - 1
    want = ((inner >> shift) << (shift + 1)) + pick * chunk + (inner & (chunk - 1))
    return jnp.where(col == want, 1.0, 0.0).astype(BF16)


def blocks_of(ref, blk):
    if len(ref.shape) == 3:
        return [ref[l] for l in range(ref.shape[0])]
    return [ref[:, l * blk : (l + 1) * blk] for l in range(ref.shape[1] // blk)]


def pack_kernel(blk, chunk, splits, spot, *refs):
    keep, send = refs[-2:]
    half = blk // 2
    pick = halves_matrix(spot[1], blk, chunk)
    at = 0
    for ref in refs[:splits]:
        for part in blocks_of(ref, blk):
            turned = mm(pick, part, NT).astype(BF16)
            keep[at] = turned[:half]
            send[at] = turned[half:]
            at += 1
    for ref in refs[splits:-2]:
        for part in blocks_of(ref, blk):
            send[at] = part[:, :half]
            send[at + 1] = part[:, half:]
            at += 2


def pack(spot, blk, chunk, name, split, whole):
    tok = split[0].shape[-2]

    def number(arrays):
        return sum(x.shape[0] if x.ndim == 3 else x.shape[1] // blk for x in arrays)

    kept, sent = number(split), number(split) + 2 * number(whole)
    return call(
        functools.partial(pack_kernel, blk, chunk, len(split)),
        name,
        (spot,) + tuple(split) + tuple(whole),
        [((kept, blk // 2, tok), BF16), ((sent, blk // 2, tok), BF16)],
        smem=1,
    )


def scatter_rows(term, spot, stage, start, chunk, first):
    for part in range(term.shape[0] // chunk):
        stage[(first + part) ^ spot, start : start + chunk] = term[
            part * chunk : (part + 1) * chunk
        ]


def flush(stage, keep, send):
    for t in range(keep.shape[0]):
        keep[t] = stage[2 * t]
        send[t] = stage[2 * t + 1]


def whole_block(ref, at):
    return jnp.concatenate([ref[at], ref[at + 1]], axis=1)


def section_term_kernel(plan, chunk, packed, spot, *refs):
    arrays, (keep, send, stage) = refs[:-3], refs[-3:]
    ups, up_come = arrays[plan["ups"]], arrays[plan["up_come"]]
    at = 0
    for up in ups:
        for l in range(up.shape[0]):
            if packed is None:
                come = up_come[0][at]
            else:
                come = whole_block(up_come[0], packed + 2 * at)
            right = jnp.concatenate([up[l], come], axis=0)
            for s in range(2):
                (mine, m), (his, h) = plan["left"][s]
                left = jnp.concatenate([arrays[mine][m + at], arrays[his][h + at]], axis=1)
                term = mm(left, right).astype(BF16)
                scatter_rows(term, spot[0], stage, (2 * at + s) * chunk, chunk, 0)
            at += 1
    flush(stage, keep, send)


def section_term(spot, name, lefts, ups, up_come, packed, chunk, groups):
    arrays, where = [], {}

    def spot_of(x):
        if id(x) not in where:
            where[id(x)] = len(arrays)
            arrays.append(x)
        return where[id(x)]

    left = [((spot_of(a), i), (spot_of(b), j)) for (a, i), (b, j) in lefts]
    first = len(arrays)
    arrays.extend(ups)
    if id(up_come) in where:
        come = where[id(up_come)]
    else:
        come = len(arrays)
        arrays.append(up_come)
    plan = {
        "left": left,
        "ups": slice(first, first + len(ups)),
        "up_come": slice(come, come + 1),
    }
    count = sum(u.shape[0] for u in ups)
    rows, wide = 2 * count * chunk, ups[0].shape[-1]
    piece = ((groups // 2, rows, wide), BF16)
    return call(
        functools.partial(section_term_kernel, plan, chunk, packed),
        name,
        (spot,) + tuple(arrays),
        [piece, piece],
        smem=1,
        scratch=(pltpu.VMEM((groups, rows, wide), BF16),),
    )


def expand_term_kernel(chunk, per, spot, keep0, come0, up, up_come, keep, send, stage):
    feats = up.shape[0] // per
    for j in range(feats):
        left = jnp.concatenate([keep0[j], come0[j]], axis=1)
        for q in range(per):
            b = j * per + q
            right = jnp.concatenate([up[b], up_come[b]], axis=0)
            term = mm(left, right).astype(BF16)
            scatter_rows(term, spot[0], stage, b * chunk, chunk, 0)
    flush(stage, keep, send)


def contract_term_kernel(chunk, cot_at, spot, keep1, come1, cot, come0, keep, send, stage):
    count, half, _ = keep1.shape
    blk = 2 * half
    feats = cot.shape[1] // blk
    per = count // feats
    for b in range(count):
        j, q = b // per, b % per
        left = jnp.concatenate([keep1[b], come1[b]], axis=1)
        right = jnp.concatenate(
            [cot[:, j * blk : (j + 1) * blk], whole_block(come0, cot_at + 2 * j)], axis=0
        )
        term = mm(left, right).astype(BF16)
        scatter_rows(term, spot[0], stage, j * chunk, chunk, q * (half // chunk))
    flush(stage, keep, send)


def output_kernel(ways, *refs):
    acts, weight, out = refs[:ways], refs[ways], refs[ways + 1]
    feats, wide, blk = weight.shape
    per = wide // blk
    blocks = [act[l] for act in acts for l in range(act.shape[0])]
    for j in range(feats):
        full = jnp.concatenate(blocks[j * per : (j + 1) * per], axis=1)
        out[:, j * blk : (j + 1) * blk] = mm(full, weight[j]).astype(BF16)


def back_kernel(section, ways, pattern, *refs):
    ups, arrived = refs[:ways], refs[ways : 2 * ways]
    weight, before, grad, outgoing, local = refs[2 * ways :]
    at = 0
    for w in range(ways):
        for l in range(ups[w].shape[0]):
            b = pattern[section, at]
            total = mm(ups[w][l], weight[at, 0], NT) + arrived[w][l].astype(F32)
            g = total.astype(BF16)
            grad[b] = g
            outgoing[b] = mm(g, before[b, 1], NT).astype(BF16)
            local[b] = mm(g, before[b, 0], NT)
            at += 1


def back_next_kernel(section, pattern, local_in, arrived, before, grad, outgoing, local):
    for at in range(local_in.shape[0]):
        b = pattern[section, at]
        g = (local_in[at] + arrived[at].astype(F32)).astype(BF16)
        grad[b] = g
        outgoing[b] = mm(g, before[b, 1], NT).astype(BF16)
        local[b] = mm(g, before[b, 0], NT)


def first_kernel(pattern, local_in, arrived, weight, grad, out):
    feats, blk, wide = weight.shape
    per = wide // blk
    for at in range(feats * per):
        b = pattern[0, at]
        grad[b] = (local_in[at] + arrived[at].astype(F32)).astype(BF16)
    for j in range(feats):
        full = jnp.concatenate([grad[j * per + q] for q in range(per)], axis=1)
        out[:, j * blk : (j + 1) * blk] = mm(full, weight[j], NT).astype(BF16)


def swap(value, axis, step):
    return lax.ppermute(value, axis, [(i, i ^ step) for i in range(lax.axis_size(axis))])


def halve(keep, send, groups):
    done = []
    bit = 1
    while True:
        come = swap(send, "dp", 2 * bit)
        done.append(come[0])
        if 2 * bit == groups:
            total = keep[0].astype(F32)
            for x in done:
                total = total + x.astype(F32)
            return total
        bit *= 2
        send = (keep[1::2].astype(F32) + come[1::2].astype(F32)).astype(BF16)
        keep = keep[0::2] if bit * 2 == groups else (keep[0::2].astype(F32) + come[0::2].astype(F32))
        if bit * 2 != groups:
            done = []


def body(tokens, expand_weight, section_weight, contract_weight, pattern, cotangent):
    rows = tokens.shape[0]
    feats, blk, wide = expand_weight.shape
    sections, count = section_weight.shape[:2]
    copies = lax.axis_size("dp")
    groups = copies // 2
    scale = 1.0 / math.sqrt(rows * copies)
    place = lax.axis_index("dp").astype(jnp.int32)
    spot = jnp.stack([place // 2, place % 2])
    narrow = blk // copies
    tall = wide // copies
    per = wide // blk
    ways = 2
    cut = count // ways
    block = (count, rows, blk)
    part = (cut, rows, blk)
    weights = [section_weight[k] for k in range(sections)]
    last = sections - 1

    place_mem = pltpu.SMEM((count,), jnp.int32)
    (chosen,) = call(
        expand_kernel, "expand", (pattern, tokens, expand_weight), [(block, BF16)],
        smem=1, scratch=(place_mem,),
    )
    saved = [tokens]
    for k in range(last):
        partner = swap(chosen, "mp", 1 << k)
        final = k + 1 == last
        outs = call(
            functools.partial(mix_kernel, k), f"mix{k}",
            (pattern, chosen, partner, weights[k]),
            [(part, BF16)] * ways if final else [(block, BF16)], smem=1,
        )
        saved += [chosen, partner]
        chosen = outs if final else outs[0]
    partners = [swap(x, "mp", 1 << last) for x in chosen]
    keep0, send0 = pack(spot, blk, narrow, "pack0", saved + list(chosen), [cotangent])
    come0 = swap(send0, "dp", 1)
    cot_at = keep0.shape[0]
    (grad_in,) = call(gelu_grad_kernel, "gelu_grad", (cotangent, contract_weight), [(block, F32)])
    acts, ups, arrived = [], [], []
    for w in range(ways):
        a, u, o = call(
            functools.partial(last_kernel, w * cut), f"last{w}",
            (chosen[w], partners[w], weights[last], grad_in), [(part, BF16)] * 3,
        )
        acts.append(a)
        ups.append(u)
        arrived.append(swap(o, "mp", 1 << last))
    keep1, send1 = pack(spot, blk, tall, "pack1", acts, [])
    come1 = swap(send1, "dp", 1)
    keep2, send2 = pack(spot, blk, narrow, "pack2", partners, ups)
    come2 = swap(send2, "dp", 1)
    (output,) = call(
        functools.partial(output_kernel, ways), "output", tuple(acts) + (contract_weight,),
        [((rows, feats * blk), BF16)],
    )
    piece = ((groups // 2, feats * tall, blk), BF16)
    contract_sum = halve(
        *call(
            functools.partial(contract_term_kernel, tall, cot_at), "contract_term",
            (spot, keep1, come1, cotangent, come0), [piece, piece], smem=1,
            scratch=(pltpu.VMEM((groups, feats * tall, blk), BF16),),
        ),
        groups,
    )
    section_sums = [None] * sections
    own_at = feats + 2 * count * last
    section_sums[last] = halve(
        *section_term(
            spot, "term_last",
            [((keep0, own_at), (come0, own_at)), ((keep2, 0), (come2, 0))],
            ups, come2, count, narrow, groups,
        ),
        groups,
    )
    local = None
    for k in range(last, 0, -1):
        if k == last:
            grad, out, local = call(
                functools.partial(back_kernel, k, ways), f"back{k}",
                (pattern,) + tuple(ups) + tuple(arrived) + (weights[k], weights[k - 1]),
                [(block, BF16), (block, BF16), (block, F32)], smem=1,
            )
        else:
            grad, out, local = call(
                functools.partial(back_next_kernel, k), f"back{k}",
                (pattern, local, come, weights[k - 1]),
                [(block, BF16), (block, BF16), (block, F32)], smem=1,
            )
        come = swap(out, "mp", 1 << (k - 1))
        grad_come = swap(grad, "dp", 1)
        own_at = feats + 2 * count * (k - 1)
        section_sums[k - 1] = halve(
            *section_term(
                spot, f"term{k - 1}",
                [((keep0, own_at), (come0, own_at)),
                 ((keep0, own_at + count), (come0, own_at + count))],
                [grad], grad_come, None, narrow, groups,
            ),
            groups,
        )
    first_grad, input_grad = call(
        first_kernel, "first", (pattern, local, come, expand_weight),
        [(block, BF16), ((rows, feats * blk), BF16)], smem=1,
    )
    first_come = swap(first_grad, "dp", 1)
    piece = ((groups // 2, count * narrow, blk), BF16)
    expand_sum = halve(
        *call(
            functools.partial(expand_term_kernel, narrow, per), "expand_term",
            (spot, keep0, come0, first_grad, first_come), [piece, piece], smem=1,
            scratch=(pltpu.VMEM((groups, count * narrow, blk), BF16),),
        ),
        groups,
    )
    section_grad = (jnp.stack(section_sums) * scale).astype(BF16)
    section_grad = section_grad.reshape(sections, count, 2, narrow, blk)
    expand_grad = (expand_sum * scale).astype(BF16)
    expand_grad = expand_grad.reshape(feats, per, narrow, blk).swapaxes(1, 2)
    expand_grad = expand_grad.reshape(feats, narrow, wide)
    contract_grad = (contract_sum * scale).astype(BF16).reshape(feats, tall, blk)
    return (output, input_grad, expand_grad, section_grad, contract_grad)


def solution(mesh):
    return jax.shard_map(
        body,
        mesh=mesh,
        in_specs=(
            P("dp", "mp"),
            P("mp", None, None),
            P(None, "mp", None, None, None),
            P("mp", None, None),
            P(),
            P("dp", "mp"),
        ),
        out_specs=(
            P("dp", "mp"),
            P("dp", "mp"),
            P("mp", "dp", None),
            P(None, "mp", None, "dp", None),
            P("mp", "dp", None),
        ),
        check_vma=False,
    )
```
